512 devices in a mesh: val: 64 (over z_hi, y, core), qry: 8 (over z_lo, x).
Axes of the slice: x: 4, y: 8, z: 8 (z_hi: 4, z_lo: 2; z = z_hi * 2 + z_lo), core: 2. Of those that a mesh axis runs over, the one named last changes fastest.
Arguments:
- queries: bfloat16 [12288, 512], P('qry'), may hold values from -20 to 20
- pool_keys: bfloat16 [32768, 512], P('val'), may hold values from -20 to 20
- pool_values: bfloat16 [32768, 512], P('val'), may hold values from -6 to 6
- out_grad: bfloat16 [12288, 512], P('qry'), may hold values from -6 to 6
- lse: float32 [2, 12288], P(None, 'qry'), as said below
- compat: int32 [2, 64, 48], P(None, 'val', 'qry'), may hold values from 0 to 1, as said below
- targets: int32 [12288, 2], P('qry'), may hold values from 0 to 32767
Outputs:
- query_grad: bfloat16 [12288, 512], P('qry')
- key_grad: bfloat16 [32768, 512], P(('val', 'qry'))
- value_grad: bfloat16 [32768, 512], P(('val', 'qry'))
The draws below stay inside these ranges and needn't reach their ends.
Inputs may be any that keep to these rules, and one draw needn't show every extreme that they name: `lse`: the forward pass's value: the log of the sum over allowed j of exp(scores[h, i, j]). `compat`: 1 where a block of 512 pool values and a block of 256 queries are type-compatible for that head.
All inputs are finite; a program needn't handle non-finite values.
Results may differ from the reference program's by a relative error of at most 0.0053.
Values may be sent and summed in bfloat16 or wider, within the bound.
A program may use at most 128 MiB of HBM per device.

```python
import jax
import jax.numpy as jnp
from jax import lax

HEADS = 2
HD = 256
VB = 512
QB = 256
QRY_DEV = 1536
VALUES = 32768
QUERIES = 12288
NVB = 64
NQB = 48


def shared_compat(key):
    block_level = jax.random.randint(jax.random.fold_in(key, 31), (HEADS, NVB, 1), 1, 5)
    mask_rolls = jax.random.randint(jax.random.fold_in(key, 32), (HEADS, NVB, NQB), 0, 8)
    return (mask_rolls < block_level).astype(jnp.int32)


def shared_targets(key):
    compat_table = shared_compat(key)
    query_block = jnp.arange(QUERIES, dtype=jnp.int32) // QB
    block_marks = jnp.transpose(compat_table, (2, 0, 1))[query_block]
    pick_score = jax.random.randint(jax.random.fold_in(key, 33), (QUERIES, HEADS, NVB), 0, 65536) * NVB + jnp.arange(NVB, dtype=jnp.int32)
    chosen = jnp.argmax(jnp.where(block_marks == 1, pick_score, -1), axis=2).astype(jnp.int32)
    inside = jax.random.randint(jax.random.fold_in(key, 34), (QUERIES, HEADS), 0, VB)
    target_ids = chosen * VB + inside
    target_ids = target_ids.at[0, 0].set(VALUES - 1)
    target_ids = target_ids.at[1, HEADS - 1].set(0)
    return target_ids.astype(jnp.int32)


def draw_queries(key, part):
    drawn_vals = jnp.clip(jax.random.normal(jax.random.fold_in(key, 51), (QUERIES, HEADS * HD), jnp.float32), -5.0, 5.0)
    return drawn_vals.astype(jnp.bfloat16)


def draw_pool_keys(key, part):
    normal_vals = jnp.clip(jax.random.normal(jax.random.fold_in(key, 61), (VALUES, HEADS * HD), jnp.float32), -5.0, 5.0)
    drawn_vals = 2.0 * normal_vals
    return drawn_vals.astype(jnp.bfloat16)


def draw_lse(key, part):
    query_all = draw_queries(key, part)
    key_all = draw_pool_keys(key, part)
    compat_table = shared_compat(key)
    target_ids = shared_targets(key)
    score_scale = HD ** (-0.5)
    block_index = jnp.arange(NVB, dtype=jnp.int32)
    head_rows = []
    for head_index in range(HEADS):
        col_low = head_index * HD
        query_head = query_all[:, col_low:col_low + HD].reshape(NQB, QB, HD)
        key_head = key_all[:, col_low:col_low + HD]
        target_head = target_ids[:, head_index].reshape(NQB, QB)
        marks = jnp.transpose(compat_table[head_index])

        def one_block(items):
            query_tile, target_tile, mark_row = items
            scores = score_scale * jnp.dot(query_tile, key_head.T, preferred_element_type=jnp.float32)
            scores = scores.reshape(QB, NVB, VB)
            usable = (mark_row[None, :] == 1) | ((target_tile // VB)[:, None] == block_index[None, :])
            usable_full = jnp.broadcast_to(usable[:, :, None], scores.shape)
            row_max = jnp.max(jnp.where(usable_full, scores, -1e+30), axis=(1, 2))
            total = jnp.sum(jnp.where(usable_full, jnp.exp(scores - row_max[:, None, None]), 0.0), axis=(1, 2))
            return row_max + jnp.log(total)
        head_rows.append(lax.map(one_block, (query_head, target_head, marks)).reshape(QUERIES))
    return jnp.stack(head_rows).astype(jnp.float32)


def draw_compat(key, part):
    return shared_compat(key)


def draw_targets(key, part):
    return shared_targets(key)


def levels(stream_key, extent, pieces, least, top_value):
    factor_of, own = 1.0, jax.random.fold_in(stream_key, 6)
    for dim, shards_of in pieces:
        steps = jnp.exp(jax.random.uniform(jax.random.fold_in(own, dim), (shards_of,), jnp.float32, least / len(pieces), top_value / len(pieces)))
        factor_of = factor_of * jnp.repeat(steps, extent[dim] // shards_of).reshape([-1 if axis == dim else 1 for axis in range(len(extent))])
    return factor_of


def scatter_about(own_key, dims, deviation, limit, split=(), held_as=jnp.bfloat16):
    drawn = jax.random.normal(own_key, dims, jnp.float32) * deviation
    if len(split) > 0:
        drawn = levels(own_key, dims, split, -0.22, 0.18) * drawn
    return jnp.clip(drawn, min=-limit, max=limit).astype(held_as)


def setup_inputs(seed: int = 0) -> dict:
    streams_of = jax.random.split(jax.random.key(seed), 8)
    queries = draw_queries(jax.random.fold_in(streams_of[7], 71), 0)
    pool_keys = draw_pool_keys(jax.random.fold_in(streams_of[7], 71), 0)
    pool_values = scatter_about(streams_of[2], (VALUES, HEADS * HD), 1.0, 6.0, ((0, 64),))
    out_grad = scatter_about(streams_of[3], (QUERIES, HEADS * HD), 1.0, 6.0, ((0, 8),))
    lse = draw_lse(jax.random.fold_in(streams_of[7], 71), 0)
    compat = draw_compat(jax.random.fold_in(streams_of[7], 71), 0)
    targets = draw_targets(jax.random.fold_in(streams_of[7], 71), 0)
    return {"queries": queries, "pool_keys": pool_keys, "pool_values": pool_values, "out_grad": out_grad, "lse": lse, "compat": compat, "targets": targets}


def reference(queries, pool_keys, pool_values, out_grad, lse, compat, targets):
    score_scale = HD ** -0.5
    block_count = QUERIES // QRY_DEV
    slot_ids = jnp.arange(VALUES, dtype=jnp.int32)
    block_index = jnp.arange(NVB, dtype=jnp.int32)
    query_outs = []
    key_outs = []
    value_outs = []
    for head_index in range(HEADS):
        col_low = head_index * HD
        key_head = pool_keys[:, col_low:col_low + HD]
        value_head = pool_values[:, col_low:col_low + HD]
        query_blocks = queries[:, col_low:col_low + HD].reshape(block_count, QRY_DEV, HD)
        grad_blocks = out_grad[:, col_low:col_low + HD].reshape(block_count, QRY_DEV, HD)
        target_blocks = targets[:, head_index].reshape(block_count, QRY_DEV)
        lse_blocks = lse[head_index].reshape(block_count, QRY_DEV)
        starts = jnp.arange(block_count, dtype=jnp.int32) * QRY_DEV
        head_marks = compat[head_index]

        def block_step(carried, block_items):
            key_acc, value_acc = carried
            query_tile, grad_tile, target_ids, lse_rows, start_row = block_items
            query_ids = start_row + jnp.arange(QRY_DEV, dtype=jnp.int32)
            per_query = jnp.transpose(head_marks[:, query_ids // QB])
            usable = (per_query == 1) | ((target_ids // VB)[:, None] == block_index[None, :])
            allowed = jnp.broadcast_to(usable[:, :, None], (QRY_DEV, NVB, VB)).reshape(QRY_DEV, VALUES)
            scores = score_scale * jnp.dot(query_tile, key_head.T, preferred_element_type=jnp.float32)
            soft_probs = jnp.where(allowed, jnp.exp(scores - lse_rows[:, None]), 0.0)
            dprobs = jnp.dot(grad_tile, value_head.T, preferred_element_type=jnp.float32)
            row_delta = jnp.sum(soft_probs * dprobs, axis=1, keepdims=True)
            onehot = (target_ids[:, None] == slot_ids[None, :]).astype(jnp.float32)
            dscores = soft_probs * (dprobs - row_delta + 1.0) - onehot
            probs_low = soft_probs.astype(jnp.bfloat16)
            dscores_low = dscores.astype(jnp.bfloat16)
            query_out = score_scale * jnp.dot(dscores_low, key_head, preferred_element_type=jnp.float32)
            key_acc = key_acc + score_scale * jnp.dot(dscores_low.T, query_tile, preferred_element_type=jnp.float32)
            value_acc = value_acc + jnp.dot(probs_low.T, grad_tile, preferred_element_type=jnp.float32)
            return (key_acc, value_acc), query_out

        start_carry = (jnp.zeros((VALUES, HD), jnp.float32), jnp.zeros((VALUES, HD), jnp.float32))
        final_carry, query_stack = lax.scan(block_step, start_carry, (query_blocks, grad_blocks, target_blocks, lse_blocks, starts))
        query_outs.append(query_stack.reshape(QUERIES, HD))
        key_outs.append(final_carry[0])
        value_outs.append(final_carry[1])
    query_grad = jnp.concatenate(query_outs, axis=1).astype(jnp.bfloat16)
    key_grad = jnp.concatenate(key_outs, axis=1).astype(jnp.bfloat16)
    value_grad = jnp.concatenate(value_outs, axis=1).astype(jnp.bfloat16)
    return (query_grad, key_grad, value_grad)
```

```python
from functools import partial

import jax
import jax.numpy as jnp
from jax import lax
from jax.experimental import pallas as pl
from jax.experimental.pallas import tpu as pltpu
from jax.sharding import PartitionSpec as P

ZH, Y, CORES, ZL, X = 4, 8, 2, 2, 4
MESH = pl.DeviceIdType.MESH
VMEM = pl.BlockSpec(memory_space=pltpu.VMEM)


def place():
    val, qry = lax.axis_index("val"), lax.axis_index("qry")
    core, y, zh = val % CORES, (val // CORES) % Y, val // (CORES * Y)
    return core, y, zh, qry // X, qry % X


def device(core, y, zh, zl, x):
    return ((zh * Y + y) * CORES + core, zl * X + x)


def neighbours():
    core, y, zh, zl, x = place()
    across = device(1 - core, y, zh, zl, x)
    along_y = [device(core, (y + d) % Y, zh, zl, x) for d in range(1, Y)]
    along_z = [device(core, y, (zh + d) % ZH, zl, x) for d in range(1, ZH)]
    along_x = [device(core, y, zh, zl, (x + d) % X) for d in range(1, X)]
    beside = device(core, y, zh, 1 - zl, x)
    return across, along_y, along_z, along_x, beside


def greet(devices):
    barrier = pltpu.get_barrier_semaphore()
    for there in devices:
        pl.semaphore_signal(barrier, inc=1, device_id=there, device_id_type=MESH)
    pl.semaphore_wait(barrier, len(devices))


def push(src, dst, send, recv, there):
    copy = pltpu.make_async_remote_copy(
        src_ref=src, dst_ref=dst, send_sem=send, recv_sem=recv, device_id=there, device_id_type=MESH
    )
    copy.start()
    return copy


def delta_kernel(part, total, from_core, sum_core, from_y, sum_y, from_z, send, recv):
    across, along_y, along_z, _, _ = neighbours()
    greet([across] + along_y + along_z)
    copies = [push(part, from_core, send.at[0], recv.at[0], across)]
    copies[0].wait_recv()
    sum_core[...] = part[...] + from_core[...]
    stage = [
        push(sum_core, from_y.at[d], send.at[1 + d], recv.at[1 + d], there)
        for d, there in enumerate(along_y)
    ]
    acc = sum_core[...]
    for d, copy in enumerate(stage):
        copy.wait_recv()
        acc = acc + from_y[d]
    sum_y[...] = acc
    copies += stage
    stage = [
        push(sum_y, from_z.at[d], send.at[Y + d], recv.at[Y + d], there)
        for d, there in enumerate(along_z)
    ]
    for d, copy in enumerate(stage):
        copy.wait_recv()
        acc = acc + from_z[d]
    total[...] = acc
    for copy in copies + stage:
        copy.wait_send()


def sum_delta(part):
    shape = part.shape
    flat = part.reshape(-1, 128)
    rows = flat.shape
    f32 = jnp.float32
    return pl.pallas_call(
        delta_kernel,
        out_shape=jax.ShapeDtypeStruct(rows, f32),
        in_specs=[VMEM],
        out_specs=VMEM,
        scratch_shapes=[
            pltpu.VMEM(rows, f32),
            pltpu.VMEM(rows, f32),
            pltpu.VMEM((Y - 1, *rows), f32),
            pltpu.VMEM(rows, f32),
            pltpu.VMEM((ZH - 1, *rows), f32),
            pltpu.SemaphoreType.DMA((Y + ZH - 1,)),
            pltpu.SemaphoreType.DMA((Y + ZH - 1,)),
        ],
        compiler_params=pltpu.CompilerParams(collective_id=0, has_side_effects=True),
    )(flat).reshape(shape)


def grads_kernel(
    query, pool, query_out, key_out, value_out,
    from_core, sum_core, from_y, sum_y, from_z, mine, line,
    from_x, sum_x, from_beside, send, recv,
):
    f32, low = jnp.float32, jnp.bfloat16
    core, y, zh, zl, x = place()
    across, along_y, along_z, along_x, beside = neighbours()
    greet([across] + along_y + along_z + along_x + [beside])
    half = from_core.shape[0]
    piece = half // Y
    width = query.shape[1] // ZH
    done = []
    used = iter(range(send.shape[0]))

    def start(src, dst, there):
        n = next(used)
        copy = push(src, dst, send.at[n], recv.at[n], there)
        done.append(copy)
        return copy

    far = pl.multiple_of((1 - core) * half, half)
    near = pl.multiple_of(core * half, half)
    swap = start(query.at[pl.ds(far, half)], from_core, across)
    x_stage = [
        start(pool.at[:, (x + d) % X], from_x.at[d - 1], there)
        for d, there in zip(range(1, X), along_x)
    ]
    swap.wait_recv()
    sum_core[...] = (query[pl.ds(near, half), :].astype(f32) + from_core[...].astype(f32)).astype(low)
    y_stage = [
        start(
            sum_core.at[pl.ds(pl.multiple_of((y + d) % Y * piece, piece), piece)],
            from_y.at[d - 1],
            there,
        )
        for d, there in zip(range(1, Y), along_y)
    ]
    acc = pool[:, x].astype(f32)
    for d, copy in enumerate(x_stage):
        copy.wait_recv()
        acc = acc + from_x[d].astype(f32)
    sum_x[...] = acc.astype(low)
    zl_copy = start(sum_x.at[1 - zl], from_beside, beside)
    acc = sum_core[pl.ds(pl.multiple_of(y * piece, piece), piece), :].astype(f32)
    for d, copy in enumerate(y_stage):
        copy.wait_recv()
        acc = acc + from_y[d].astype(f32)
    sum_y[...] = acc.astype(low)
    z_stage = [
        start(
            sum_y.at[:, pl.ds(pl.multiple_of((zh + d) % ZH * width, width), width)],
            from_z.at[d - 1],
            there,
        )
        for d, there in zip(range(1, ZH), along_z)
    ]
    zl_copy.wait_recv()
    pool_sum = (sum_x[zl].astype(f32) + from_beside[...].astype(f32)).astype(low)
    split = pool_sum.shape[1] // 2
    key_out[...] = pool_sum[:, :split]
    value_out[...] = pool_sum[:, split:]
    own_columns = pl.ds(pl.multiple_of(zh * width, width), width)
    acc = sum_y[:, own_columns].astype(f32)
    for d, copy in enumerate(z_stage):
        copy.wait_recv()
        acc = acc + from_z[d].astype(f32)
    mine[...] = acc.astype(low)
    back_z = [start(mine, line.at[:, own_columns], there) for there in along_z]
    line[:, own_columns] = mine[...]
    for copy in back_z:
        copy.wait_recv()
    own_rows = pl.ds(pl.multiple_of(core * half + y * piece, piece), piece)
    back_y = [start(line, query_out.at[own_rows], there) for there in along_y]
    query_out[own_rows, :] = line[...]
    back_core = [start(line, query_out.at[own_rows], across)]
    for d, copy in zip(range(1, Y), back_y):
        copy.wait_recv()
        rows = pl.ds(pl.multiple_of(core * half + (y + Y - d) % Y * piece, piece), piece)
        back_core.append(start(query_out.at[rows], query_out.at[rows], across))
    for copy in back_core:
        copy.wait_recv()
    for copy in done:
        copy.wait_send()


def sum_grads(query, pool):
    low = jnp.bfloat16
    count, columns = query.shape
    rows, wide = pool.shape
    share = rows // (ZL * X)
    half = count // CORES
    piece = half // Y
    width = columns // ZH
    copies = 1 + (X - 1) + (Y - 1) + 1 + (ZH - 1) * 2 + (Y - 1) + Y
    return pl.pallas_call(
        grads_kernel,
        out_shape=(
            jax.ShapeDtypeStruct(query.shape, low),
            jax.ShapeDtypeStruct((share, wide // 2), low),
            jax.ShapeDtypeStruct((share, wide // 2), low),
        ),
        in_specs=[VMEM, VMEM],
        out_specs=(VMEM, VMEM, VMEM),
        scratch_shapes=[
            pltpu.VMEM((half, columns), low),
            pltpu.VMEM((half, columns), low),
            pltpu.VMEM((Y - 1, piece, columns), low),
            pltpu.VMEM((piece, columns), low),
            pltpu.VMEM((ZH - 1, piece, width), low),
            pltpu.VMEM((piece, width), low),
            pltpu.VMEM((piece, columns), low),
            pltpu.VMEM((X - 1, ZL, share, wide), low),
            pltpu.VMEM((ZL, share, wide), low),
            pltpu.VMEM((share, wide), low),
            pltpu.SemaphoreType.DMA((copies,)),
            pltpu.SemaphoreType.DMA((copies,)),
        ],
        compiler_params=pltpu.CompilerParams(collective_id=1, has_side_effects=True),
    )(query, pool.reshape(ZL, X, share, wide))


def on_device(queries, pool_keys, pool_values, out_grad, lse, compat, targets):
    num_heads = compat.shape[0]
    head_width = queries.shape[1] // num_heads
    query_count = queries.shape[0]
    value_count = pool_keys.shape[0]
    value_blocks = compat.shape[1]
    query_block = query_count // compat.shape[2]
    value_block = value_count // value_blocks
    score_scale = head_width ** (-0.5)
    value_index = lax.axis_index("val")
    offset = value_index * value_count
    block_ids = value_index * value_blocks + jnp.arange(value_blocks, dtype=jnp.int32)
    positions = jnp.arange(value_count, dtype=jnp.int32)

    def head_slices(head_index, first_row):
        col_low = head_index * head_width
        query_tile = queries[first_row : first_row + query_count, col_low : col_low + head_width]
        grad_tile = out_grad[first_row : first_row + query_count, col_low : col_low + head_width]
        return (
            query_tile,
            grad_tile,
            pool_keys[:, col_low : col_low + head_width],
            pool_values[:, col_low : col_low + head_width],
        )

    def first_pass(head_index, first_row, allowed):
        query_tile, grad_tile, key_head, value_head = head_slices(head_index, first_row)
        scores = score_scale * jnp.einsum(
            "qd,kd->qk", query_tile, key_head, preferred_element_type=jnp.float32
        )
        dprobs = jnp.einsum("qd,kd->qk", grad_tile, value_head, preferred_element_type=jnp.float32)
        lse_rows = lse[head_index, first_row : first_row + query_count]
        soft_probs = jnp.where(allowed, jnp.exp(scores - lse_rows[:, None]), 0.0)
        return (soft_probs, dprobs)

    records = []
    for head_index in range(num_heads):
        first_row = 0
        target_ids = targets[first_row : first_row + query_count, head_index]
        block_marks = compat[
            head_index, :, first_row // query_block : (first_row + query_count) // query_block
        ]
        per_query = jnp.broadcast_to(
            jnp.transpose(block_marks)[:, None, :],
            (query_count // query_block, query_block, value_blocks),
        ).reshape(query_count, value_blocks)
        target_hits = (target_ids // value_block)[:, None] == block_ids[None, :]
        usable = (per_query == 1) | target_hits
        layout_allowed = jnp.broadcast_to(
            usable[:, :, None], (query_count, value_blocks, value_block)
        ).reshape(query_count, value_count)
        onehot = ((target_ids - offset)[:, None] == positions[None, :]).astype(jnp.float32)
        allowed, onehot, is_live = (layout_allowed, onehot, jnp.any(usable))
        compute = partial(first_pass, head_index, first_row, allowed)
        outcome = compute()
        records.append((head_index, first_row, allowed, onehot, is_live, outcome))
    local_delta = jnp.stack(
        [
            jnp.concatenate(
                [
                    jnp.sum(record[5][0] * record[5][1], axis=1)
                    for record in records
                    if record[0] == head_index
                ]
            )
            for head_index in range(num_heads)
        ]
    )
    row_delta = sum_delta(local_delta)

    def second_pass(head_index, first_row, soft_probs, dprobs, onehot):
        query_tile, grad_tile, key_head, value_head = head_slices(head_index, first_row)
        delta_rows = row_delta[head_index, first_row : first_row + query_count]
        dscores = soft_probs * (dprobs - delta_rows[:, None] + 1.0) - onehot
        probs_low = soft_probs.astype(jnp.bfloat16)
        dscores_low = dscores.astype(jnp.bfloat16)
        query_term = score_scale * jnp.einsum(
            "qk,kd->qd", dscores_low, key_head, preferred_element_type=jnp.float32
        )
        key_term = score_scale * jnp.einsum(
            "qk,qd->kd", dscores_low, query_tile, preferred_element_type=jnp.float32
        )
        value_term = jnp.einsum(
            "qk,qd->kd", probs_low, grad_tile, preferred_element_type=jnp.float32
        )
        return (query_term, key_term, value_term)

    query_lists = [[] for head_index in range(num_heads)]
    key_sums = [
        jnp.zeros((value_count, head_width), jnp.float32) for head_index in range(num_heads)
    ]
    value_sums = [
        jnp.zeros((value_count, head_width), jnp.float32) for head_index in range(num_heads)
    ]
    for record in records:
        compute = partial(second_pass, record[0], record[1], record[5][0], record[5][1], record[3])
        outcome = compute()
        query_lists[record[0]].append(outcome[0])
        key_sums[record[0]] = outcome[1]
        value_sums[record[0]] = outcome[2]
    query_part = jnp.concatenate([pieces[0] for pieces in query_lists], axis=1)
    pool_part = jnp.concatenate(key_sums + value_sums, axis=1)
    return sum_grads(query_part.astype(jnp.bfloat16), pool_part.astype(jnp.bfloat16))


def solution(mesh):
    placed = (
        P("qry", None),
        P("val", None),
        P("val", None),
        P("qry", None),
        P(None, "qry"),
        P(None, "val", "qry"),
        P("qry", None),
    )
    return jax.shard_map(
        on_device,
        mesh=mesh,
        in_specs=placed,
        out_specs=(P("qry", None), P(("val", "qry"), None), P(("val", "qry"), None)),
        check_vma=False,
    )
```

```python
import jax
import jax.numpy as jnp
from jax import lax
from jax.experimental import pallas as pl
from jax.experimental.pallas import tpu as pltpu
from jax.sharding import PartitionSpec as P

ZH, Y, CORES, ZL, X = 4, 8, 2, 2, 4
UP, DOWN = 4, 3
CHUNKS, POOL_WAIT = 2, 4
MESH = pl.DeviceIdType.MESH
VMEM = pl.BlockSpec(memory_space=pltpu.VMEM)


def place():
    val, qry = lax.axis_index("val"), lax.axis_index("qry")
    core, y, zh = val % CORES, (val // CORES) % Y, val // (CORES * Y)
    return core, y, zh, qry // X, qry % X


def device(core, y, zh, zl, x):
    return ((zh * Y + y) * CORES + core, zl * X + x)


def neighbours():
    core, y, zh, zl, x = place()
    across = device(1 - core, y, zh, zl, x)
    along_y = [device(core, (y + d) % Y, zh, zl, x) for d in range(1, Y)]
    along_z = [device(core, y, (zh + d) % ZH, zl, x) for d in range(1, ZH)]
    along_x = [device(core, y, zh, zl, (x + d) % X) for d in range(1, X)]
    beside = device(core, y, zh, 1 - zl, x)
    return across, along_y, along_z, along_x, beside


def mult(first, size):
    return pl.ds(pl.multiple_of(first, size), size)


def dot(a, b, dims):
    return lax.dot_general(a, b, ((dims[:1], dims[1:]), ((), ())), preferred_element_type=jnp.float32)


def push(src, dst, send, recv, there):
    copy = pltpu.make_async_remote_copy(
        src_ref=src, dst_ref=dst, send_sem=send, recv_sem=recv, device_id=there, device_id_type=MESH
    )
    copy.start()
    return copy


def backward_kernel(
    queries, grads, keys, values, lse, local, query_out, key_out, value_out,
    probs, weights, delta, delta_core, delta_sum, delta_y, delta_line, delta_z, query, sums, key_sums, pool,
    from_core, up_in, down_in, up_out, down_out, sum_y, from_z, mine, line,
    from_x, sum_x, from_beside, send, recv,
):
    f32, low = jnp.float32, jnp.bfloat16
    core, y, zh, zl, x = place()
    across, along_y, along_z, along_x, beside = neighbours()
    upper, lower = along_y[0], along_y[-1]
    friends = [across] + along_y + along_z + along_x + [beside]
    barrier = pltpu.get_barrier_semaphore()
    for there in friends:
        pl.semaphore_signal(barrier, inc=1, device_id=there, device_id_type=MESH)

    count, columns = queries.shape
    tiles, tile = lse.shape
    heads = probs.shape[0]
    head_width = columns // heads
    per_head = tiles // heads
    scale = head_width ** (-0.5)
    half = from_core.shape[1]
    piece = half // Y
    width = columns // ZH
    share = key_out.shape[0]
    own_columns = mult(zh * width, width)
    done = []
    used = iter(range(send.shape[0]))

    def start(src, dst, there):
        n = next(used)
        copy = push(src, dst, send.at[n], recv.at[n], there)
        done.append(copy)
        return copy

    def head_columns(h):
        return pl.ds(h * head_width, head_width)

    for h in range(heads):
        cols = head_columns(h)
        sums[...] = jnp.zeros_like(sums)

        def first_pass(b, carry):
            rows = mult(b * tile, tile)
            grad_tile = grads[rows, cols]
            scores = dot(keys[:, cols], queries[rows, cols], (1, 1)) * scale
            p = jnp.exp(scores - lse[pl.ds(h * per_head + b, 1), :])
            dprobs = dot(values[:, cols], grad_tile, (1, 1))
            terms = p * dprobs
            delta[pl.ds(h * per_head + b, 1), :] = jnp.sum(terms, axis=0, keepdims=True)
            slot = lax.broadcasted_iota(jnp.int32, p.shape, 0)
            hit = slot == local[pl.ds(h * per_head + b, 1), :]
            probs[h, :, rows] = p
            weights[h, :, rows] = terms + p - jnp.where(hit, 1.0, 0.0)
            sums[...] += dot(p.astype(low), grad_tile, (1, 0))
            return carry

        lax.fori_loop(0, per_head, first_pass, 0)
        for r in range(ZL * X):
            pool[1, r // X, r % X, :, cols] = sums[pl.ds(r * share, share), :].astype(low)

    pl.semaphore_wait(barrier, len(friends))

    def pool_steps(n, out, wait):
        x_stage = [
            start(pool.at[n, :, (x + d) % X], from_x.at[n, d - 1], there)
            for d, there in zip(range(1, X), along_x)
        ]
        for _ in range(wait):
            yield
        acc = pool[n, :, x].astype(f32)
        for d, copy in enumerate(x_stage):
            copy.wait_recv()
            acc = acc + from_x[n, d].astype(f32)
        sum_x[n] = acc.astype(low)
        copy = start(sum_x.at[n, 1 - zl], from_beside.at[n], beside)
        for _ in range(3):
            yield
        copy.wait_recv()
        out[...] = (sum_x[n, zl].astype(f32) + from_beside[n].astype(f32)).astype(low)

    swap = start(delta, delta_core, across)
    swap.wait_recv()
    delta_sum[...] = delta[...] + delta_core[...]
    stage = [start(delta_sum, delta_y.at[d], there) for d, there in enumerate(along_y)]
    value_lane = pool_steps(1, value_out, 1)
    next(value_lane)
    acc = delta_sum[...]
    for d, copy in enumerate(stage):
        copy.wait_recv()
        acc = acc + delta_y[d]
    delta_line[...] = acc
    stage = [start(delta_line, delta_z.at[d], there) for d, there in enumerate(along_z)]
    for d, copy in enumerate(stage):
        copy.wait_recv()
        acc = acc + delta_z[d]
    delta_core[...] = acc

    def rows(k, c, owner):
        first = k * CORES * half + c * half + lax.rem(owner + Y, Y) * piece
        return pl.ds(pl.multiple_of(first, piece), piece)

    def half_rows(k, c):
        return pl.ds(pl.multiple_of(k * CORES * half + c * half, half), half)

    def own(k, owner):
        inside = pl.ds(pl.multiple_of(lax.rem(owner + Y, Y) * piece, piece), piece)
        return query[rows(k, core, owner), :].astype(f32) + from_core[k, inside, :].astype(f32)

    def query_steps(k):
        swap = start(query.at[half_rows(k, 1 - core)], from_core.at[k], across)
        yield
        swap.wait_recv()
        up_out[k, 0] = own(k, y + UP).astype(low)
        up = start(up_out.at[k, 0], up_in.at[k, 0], upper)
        down_out[k, 0] = own(k, y - DOWN).astype(low)
        down = start(down_out.at[k, 0], down_in.at[k, 0], lower)
        for s in range(1, UP):
            yield
            up.wait_recv()
            up_out[k, s] = (own(k, y + UP - s) + up_in[k, s - 1].astype(f32)).astype(low)
            up = start(up_out.at[k, s], up_in.at[k, s], upper)
            if s < DOWN:
                down.wait_recv()
                down_out[k, s] = (own(k, y - DOWN + s) + down_in[k, s - 1].astype(f32)).astype(low)
                down = start(down_out.at[k, s], down_in.at[k, s], lower)
        yield
        down.wait_recv()
        up.wait_recv()
        total = own(k, y) + up_in[k, UP - 1].astype(f32) + down_in[k, DOWN - 1].astype(f32)
        sum_y[k] = total.astype(low)
        z_stage = [
            start(
                sum_y.at[k, :, pl.ds(pl.multiple_of((zh + d) % ZH * width, width), width)],
                from_z.at[k, d - 1],
                there,
            )
            for d, there in zip(range(1, ZH), along_z)
        ]
        yield
        acc = sum_y[k, :, own_columns].astype(f32)
        for d, copy in enumerate(z_stage):
            copy.wait_recv()
            acc = acc + from_z[k, d].astype(f32)
        mine[k] = acc.astype(low)
        back_z = [start(mine.at[k], line.at[k, :, own_columns], there) for there in along_z]
        line[k, :, own_columns] = mine[k]
        yield
        for copy in back_z:
            copy.wait_recv()
        here = rows(k, core, y)
        up = start(line.at[k], query_out.at[here], upper)
        down = start(line.at[k], query_out.at[here], lower)
        query_out[here, :] = line[k]
        back_core = [start(line.at[k], query_out.at[here], across)]
        for s in range(1, UP + 1):
            yield
            up.wait_recv()
            got = query_out.at[rows(k, core, y - s)]
            if s < UP:
                up = start(got, got, upper)
            forward = [got]
            if s <= DOWN:
                down.wait_recv()
                got = query_out.at[rows(k, core, y + s)]
                if s < DOWN:
                    down = start(got, got, lower)
                forward.append(got)
            back_core += [start(got, got, across) for got in forward]
        yield
        for copy in back_core:
            copy.wait_recv()

    def second_pass(k, h):
        cols = head_columns(h)

        def step(b, carry):
            rows = mult(b * tile, tile)
            d = delta_core[pl.ds(h * per_head + b, 1), :]
            dscores = (weights[h, :, rows] - probs[h, :, rows] * d).astype(low)
            query[rows, cols] = (dot(dscores, keys[:, cols], (0, 0)) * scale).astype(low)
            key_sums[:, cols] += dot(dscores, queries[rows, cols], (1, 0))
            return carry

        per_chunk = per_head // CHUNKS
        lax.fori_loop(k * per_chunk, (k + 1) * per_chunk, step, 0)

    key_sums[...] = jnp.zeros_like(key_sums)
    lanes = [value_lane]
    for k in range(CHUNKS):
        for h in range(heads):
            second_pass(k, h)
        lanes.append(query_steps(k))
        next(lanes[-1])
    for r in range(ZL * X):
        pool[0, r // X, r % X] = (key_sums[pl.ds(r * share, share), :] * scale).astype(low)
    lanes.append(pool_steps(0, key_out, POOL_WAIT))
    while lanes:
        lanes = [steps for steps in lanes if next(steps, lanes) is not lanes]
    for copy in done:
        copy.wait_send()


def on_device(queries, pool_keys, pool_values, out_grad, lse, compat, targets):
    heads, value_blocks, query_blocks = compat.shape
    count, columns = queries.shape
    value_count = pool_keys.shape[0]
    val = lax.axis_index("val")
    query_block = count // query_blocks
    tiles = heads * query_blocks
    low, f32 = jnp.bfloat16, jnp.float32
    wanted = jnp.transpose(targets)
    marks = jnp.repeat(compat[:, 0, :], query_block, axis=1)
    usable = (marks == 1) | (wanted // value_count == val)
    lse_rows = jnp.where(usable, lse, 3e38).reshape(tiles, query_block)
    local = (wanted - val * value_count).reshape(tiles, query_block)
    share = value_count // (ZL * X)
    half = count // (CORES * CHUNKS)
    piece = half // Y
    width = columns // ZH
    copies = CHUNKS * (1 + (Y - 1) + (ZH - 1) * 2 + (Y - 1) + Y) + 2 * X + 1 + (Y - 1) + (ZH - 1)
    row = (tiles, query_block)
    return pl.pallas_call(
        backward_kernel,
        out_shape=(
            jax.ShapeDtypeStruct(queries.shape, low),
            jax.ShapeDtypeStruct((share, columns), low),
            jax.ShapeDtypeStruct((share, columns), low),
        ),
        in_specs=[VMEM] * 6,
        out_specs=(VMEM, VMEM, VMEM),
        scratch_shapes=[
            pltpu.VMEM((heads, value_count, count), f32),
            pltpu.VMEM((heads, value_count, count), f32),
            pltpu.VMEM(row, f32),
            pltpu.VMEM(row, f32),
            pltpu.VMEM(row, f32),
            pltpu.VMEM((Y - 1, *row), f32),
            pltpu.VMEM(row, f32),
            pltpu.VMEM((ZH - 1, *row), f32),
            pltpu.VMEM(queries.shape, low),
            pltpu.VMEM((value_count, columns // heads), f32),
            pltpu.VMEM((value_count, columns), f32),
            pltpu.VMEM((2, ZL, X, share, columns), low),
            pltpu.VMEM((CHUNKS, half, columns), low),
            pltpu.VMEM((CHUNKS, UP, piece, columns), low),
            pltpu.VMEM((CHUNKS, DOWN, piece, columns), low),
            pltpu.VMEM((CHUNKS, UP, piece, columns), low),
            pltpu.VMEM((CHUNKS, DOWN, piece, columns), low),
            pltpu.VMEM((CHUNKS, piece, columns), low),
            pltpu.VMEM((CHUNKS, ZH - 1, piece, width), low),
            pltpu.VMEM((CHUNKS, piece, width), low),
            pltpu.VMEM((CHUNKS, piece, columns), low),
            pltpu.VMEM((2, X - 1, ZL, share, columns), low),
            pltpu.VMEM((2, ZL, share, columns), low),
            pltpu.VMEM((2, share, columns), low),
            pltpu.SemaphoreType.DMA((copies,)),
            pltpu.SemaphoreType.DMA((copies,)),
        ],
        compiler_params=pltpu.CompilerParams(
            collective_id=0, has_side_effects=True, vmem_limit_bytes=56 * 1024 * 1024
        ),
    )(queries, out_grad, pool_keys, pool_values, lse_rows, local)


def solution(mesh):
    placed = (
        P("qry", None),
        P("val", None),
        P("val", None),
        P("qry", None),
        P(None, "qry"),
        P(None, "val", "qry"),
        P("qry", None),
    )
    return jax.shard_map(
        on_device,
        mesh=mesh,
        in_specs=placed,
        out_specs=(P("qry", None), P(("val", "qry"), None), P(("val", "qry"), None)),
        check_vma=False,
    )
```

```python
import jax
import jax.numpy as jnp
from jax import lax
from jax.experimental import pallas as pl
from jax.experimental.pallas import tpu as pltpu
from jax.sharding import PartitionSpec as P

ZH, Y, CORES, ZL, X = 4, 8, 2, 2, 4
UP, DOWN = 4, 3
POOL_WAIT = 4
MESH = pl.DeviceIdType.MESH
VMEM = pl.BlockSpec(memory_space=pltpu.VMEM)


def place():
    val, qry = lax.axis_index("val"), lax.axis_index("qry")
    core, y, zh = val % CORES, (val // CORES) % Y, val // (CORES * Y)
    return core, y, zh, qry // X, qry % X


def device(core, y, zh, zl, x):
    return ((zh * Y + y) * CORES + core, zl * X + x)


def neighbours():
    core, y, zh, zl, x = place()
    across = device(1 - core, y, zh, zl, x)
    along_y = [device(core, (y + d) % Y, zh, zl, x) for d in range(1, Y)]
    along_z = [device(core, y, (zh + d) % ZH, zl, x) for d in range(1, ZH)]
    along_x = [device(core, y, zh, zl, (x + d) % X) for d in range(1, X)]
    beside = device(core, y, zh, 1 - zl, x)
    return across, along_y, along_z, along_x, beside


def mult(first, size):
    return pl.ds(pl.multiple_of(first, size), size)


def dot(a, b, dims):
    return lax.dot_general(a, b, ((dims[:1], dims[1:]), ((), ())), preferred_element_type=jnp.float32)


def push(src, dst, send, recv, there):
    copy = pltpu.make_async_remote_copy(
        src_ref=src, dst_ref=dst, send_sem=send, recv_sem=recv, device_id=there, device_id_type=MESH
    )
    copy.start()
    return copy


def backward_kernel(
    queries, grads, keys, values, lse, targets, compat, query_out, key_out, value_out,
    probs, weights, delta, delta_core, delta_sum, delta_y, delta_line, delta_z, query, sums, pool,
    from_core, up_in, down_in, up_out, down_out, sum_y, from_z, mine, line, whole,
    from_x, sum_x, from_beside, send, recv,
):
    f32, low = jnp.float32, jnp.bfloat16
    core, y, zh, zl, x = place()
    across, along_y, along_z, along_x, beside = neighbours()
    upper, lower = along_y[0], along_y[-1]
    friends = [across] + along_y + along_z + along_x + [beside]
    barrier = pltpu.get_barrier_semaphore()
    for there in friends:
        pl.semaphore_signal(barrier, inc=1, device_id=there, device_id_type=MESH)

    heads, per_head, tile = delta.shape
    count, columns = queries.shape
    value_count = keys.shape[0]
    head_width = columns // heads
    scale = head_width ** (-0.5)
    half = from_core.shape[1]
    piece = half // Y
    part = piece // ZH
    share = key_out.shape[0]
    offset = lax.axis_index("val") * value_count
    done = []
    used = iter(range(send.shape[0]))

    def start(src, dst, there):
        n = next(used)
        copy = push(src, dst, send.at[n], recv.at[n], there)
        done.append(copy)
        return copy

    def head_columns(h):
        return pl.ds(h * head_width, head_width)

    def first_pass(h, low_tile, high_tile):
        cols = head_columns(h)

        def step(b, carry):
            rows = mult(b * tile, tile)
            grad_tile = grads[rows, cols]
            local = targets[pl.ds(h, 1), rows] - offset
            mark = jnp.full(local.shape, compat[h, b], jnp.int32)
            usable = (mark == 1) | ((local >= 0) & (local < value_count))
            lse_row = jnp.where(usable, lse[pl.ds(h, 1), rows], 3e38)
            scores = dot(keys[:, cols], queries[rows, cols], (1, 1)) * scale
            p = jnp.exp(scores - lse_row)
            dprobs = dot(values[:, cols], grad_tile, (1, 1))
            terms = p * dprobs
            delta[h, pl.ds(b, 1), :] = jnp.sum(terms, axis=0, keepdims=True)
            hit = lax.broadcasted_iota(jnp.int32, p.shape, 0) == local
            probs[h, :, rows] = p
            weights[h, :, rows] = terms + p - jnp.where(hit, 1.0, 0.0)
            sums[1, h] += dot(p.astype(low), grad_tile, (1, 0))
            return carry

        lax.fori_loop(low_tile, high_tile, step, 0)

    def second_pass(h, low_tile, high_tile):
        cols = head_columns(h)

        def step(b, carry):
            rows = mult(b * tile, tile)
            d = delta_core[h, pl.ds(b, 1), :]
            dscores = (weights[h, :, rows] - probs[h, :, rows] * d).astype(low)
            query[h, rows, :] = (dot(dscores, keys[:, cols], (0, 0)) * scale).astype(low)
            sums[0, h] += dot(dscores, queries[rows, cols], (1, 0))
            return carry

        lax.fori_loop(low_tile, high_tile, step, 0)

    def delta_steps(h):
        swap = start(delta.at[h], delta_core.at[h], across)
        yield
        swap.wait_recv()
        delta_sum[h] = delta[h] + delta_core[h]
        stage = [start(delta_sum.at[h], delta_y.at[h, d], there) for d, there in enumerate(along_y)]
        yield
        acc = delta_sum[h]
        for d, copy in enumerate(stage):
            copy.wait_recv()
            acc = acc + delta_y[h, d]
        delta_line[h] = acc
        stage = [start(delta_line.at[h], delta_z.at[h, d], there) for d, there in enumerate(along_z)]
        yield
        for d, copy in enumerate(stage):
            copy.wait_recv()
            acc = acc + delta_z[h, d]
        delta_core[h] = acc

    def pool_steps(n, h, out, factor, wait):
        for r in range(ZL * X):
            pool[n, h, r // X, r % X] = (sums[n, h, pl.ds(r * share, share), :] * factor).astype(low)
        x_stage = [
            start(pool.at[n, h, :, (x + d) % X], from_x.at[n, h, d - 1], there)
            for d, there in zip(range(1, X), along_x)
        ]
        for _ in range(wait):
            yield
        acc = pool[n, h, :, x].astype(f32)
        for d, copy in enumerate(x_stage):
            copy.wait_recv()
            acc = acc + from_x[n, h, d].astype(f32)
        sum_x[n, h] = acc.astype(low)
        copy = start(sum_x.at[n, h, 1 - zl], from_beside.at[n, h], beside)
        for _ in range(3):
            yield
        copy.wait_recv()
        out[:, head_columns(h)] = (sum_x[n, h, zl].astype(f32) + from_beside[n, h].astype(f32)).astype(low)

    def query_steps(h):
        cols = head_columns(h)

        def rows(c, owner):
            return mult(c * half + lax.rem(owner + Y, Y) * piece, piece)

        def own(owner):
            inside = mult(lax.rem(owner + Y, Y) * piece, piece)
            return query[h, rows(core, owner), :].astype(f32) + from_core[h, inside, :].astype(f32)

        swap = start(query.at[h, mult((1 - core) * half, half)], from_core.at[h], across)
        yield
        swap.wait_recv()
        up_out[h, 0] = own(y + UP).astype(low)
        up = start(up_out.at[h, 0], up_in.at[h, 0], upper)
        down_out[h, 0] = own(y - DOWN).astype(low)
        down = start(down_out.at[h, 0], down_in.at[h, 0], lower)
        for s in range(1, UP):
            yield
            up.wait_recv()
            up_out[h, s] = (own(y + UP - s) + up_in[h, s - 1].astype(f32)).astype(low)
            up = start(up_out.at[h, s], up_in.at[h, s], upper)
            if s < DOWN:
                down.wait_recv()
                down_out[h, s] = (own(y - DOWN + s) + down_in[h, s - 1].astype(f32)).astype(low)
                down = start(down_out.at[h, s], down_in.at[h, s], lower)
        yield
        down.wait_recv()
        up.wait_recv()
        total = own(y) + up_in[h, UP - 1].astype(f32) + down_in[h, DOWN - 1].astype(f32)
        for r in range(ZH):
            sum_y[h, r] = total[r * part : (r + 1) * part].astype(low)
        z_stage = [
            start(sum_y.at[h, (zh + d) % ZH], from_z.at[h, d - 1], there)
            for d, there in zip(range(1, ZH), along_z)
        ]
        yield
        acc = sum_y[h, zh].astype(f32)
        for d, copy in enumerate(z_stage):
            copy.wait_recv()
            acc = acc + from_z[h, d].astype(f32)
        mine[h] = acc.astype(low)
        back_z = [start(mine.at[h], line.at[h, zh], there) for there in along_z]
        line[h, zh] = mine[h]
        yield
        for copy in back_z:
            copy.wait_recv()
        whole[h] = jnp.concatenate([line[h, r].astype(f32) for r in range(ZH)], axis=0).astype(low)
        here = query_out.at[rows(core, y), cols]
        up = start(whole.at[h], here, upper)
        down = start(whole.at[h], here, lower)
        back_core = [start(whole.at[h], here, across)]
        query_out[rows(core, y), cols] = whole[h]
        for s in range(1, UP + 1):
            yield
            up.wait_recv()
            got = query_out.at[rows(core, y - s), cols]
            if s < UP:
                up = start(got, got, upper)
            forward = [got]
            if s <= DOWN:
                down.wait_recv()
                got = query_out.at[rows(core, y + s), cols]
                if s < DOWN:
                    down = start(got, got, lower)
                forward.append(got)
            back_core += [start(got, got, across) for got in forward]
        yield
        for copy in back_core:
            copy.wait_recv()

    sums[...] = jnp.zeros_like(sums)
    mid = per_head // 2
    first_pass(0, 0, per_head)
    pl.semaphore_wait(barrier, len(friends))
    delta_lane = delta_steps(0)
    next(delta_lane)
    lanes = [pool_steps(1, 0, value_out, 1.0, 2)]
    next(lanes[0])
    first_pass(1, 0, mid)
    next(delta_lane)
    first_pass(1, mid, per_head)
    later_lane = delta_steps(1)
    next(later_lane)
    next(delta_lane)
    lanes.append(pool_steps(1, 1, value_out, 1.0, 2))
    next(lanes[1])
    next(later_lane)
    next(delta_lane, None)
    second_pass(0, 0, per_head)
    ahead = query_steps(0)
    next(ahead)
    next(later_lane)
    lanes.append(pool_steps(0, 0, key_out, scale, POOL_WAIT))
    next(lanes[2])
    next(ahead)
    next(later_lane, None)
    for b in range(0, per_head, 2):
        second_pass(1, b, b + 2)
        if b + 2 < per_head:
            next(ahead)
    behind = query_steps(1)
    next(behind)
    lanes = [ahead, behind] + lanes + [pool_steps(0, 1, key_out, scale, POOL_WAIT)]
    while lanes:
        lanes = [steps for steps in lanes if next(steps, lanes) is not lanes]
    for copy in done:
        copy.wait_send()


def on_device(queries, pool_keys, pool_values, out_grad, lse, compat, targets):
    heads, _, query_blocks = compat.shape
    count, columns = queries.shape
    value_count = pool_keys.shape[0]
    low, f32 = jnp.bfloat16, jnp.float32
    share = value_count // (ZL * X)
    half = count // CORES
    piece = half // Y
    part = piece // ZH
    wide = columns // heads
    copies = heads * (1 + (Y - 1) + (ZH - 1) * 2 + (Y - 1) + Y + 2 * X + 1 + (Y - 1) + (ZH - 1))
    row = (query_blocks, count // query_blocks)
    return pl.pallas_call(
        backward_kernel,
        out_shape=(
            jax.ShapeDtypeStruct(queries.shape, low),
            jax.ShapeDtypeStruct((share, columns), low),
            jax.ShapeDtypeStruct((share, columns), low),
        ),
        in_specs=[VMEM] * 6 + [pl.BlockSpec(memory_space=pltpu.SMEM)],
        out_specs=(VMEM, VMEM, VMEM),
        scratch_shapes=[
            pltpu.VMEM((heads, value_count, count), f32),
            pltpu.VMEM((heads, value_count, count), f32),
            pltpu.VMEM((heads, *row), f32),
            pltpu.VMEM((heads, *row), f32),
            pltpu.VMEM((heads, *row), f32),
            pltpu.VMEM((heads, Y - 1, *row), f32),
            pltpu.VMEM((heads, *row), f32),
            pltpu.VMEM((heads, ZH - 1, *row), f32),
            pltpu.VMEM((heads, count, wide), low),
            pltpu.VMEM((2, heads, value_count, wide), f32),
            pltpu.VMEM((2, heads, ZL, X, share, wide), low),
            pltpu.VMEM((heads, half, wide), low),
            pltpu.VMEM((heads, UP, piece, wide), low),
            pltpu.VMEM((heads, DOWN, piece, wide), low),
            pltpu.VMEM((heads, UP, piece, wide), low),
            pltpu.VMEM((heads, DOWN, piece, wide), low),
            pltpu.VMEM((heads, ZH, part, wide), low),
            pltpu.VMEM((heads, ZH - 1, part, wide), low),
            pltpu.VMEM((heads, part, wide), low),
            pltpu.VMEM((heads, ZH, part, wide), low),
            pltpu.VMEM((heads, piece, wide), low),
            pltpu.VMEM((2, heads, X - 1, ZL, share, wide), low),
            pltpu.VMEM((2, heads, ZL, share, wide), low),
            pltpu.VMEM((2, heads, share, wide), low),
            pltpu.SemaphoreType.DMA((copies,)),
            pltpu.SemaphoreType.DMA((copies,)),
        ],
        compiler_params=pltpu.CompilerParams(
            collective_id=0, has_side_effects=True, vmem_limit_bytes=56 * 1024 * 1024
        ),
    )(queries, out_grad, pool_keys, pool_values, lse, jnp.transpose(targets), compat[:, 0, :])


def solution(mesh):
    placed = (
        P("qry", None),
        P("val", None),
        P("val", None),
        P("qry", None),
        P(None, "qry"),
        P(None, "val", "qry"),
        P("qry", None),
    )
    return jax.shard_map(
        on_device,
        mesh=mesh,
        in_specs=placed,
        out_specs=(P("qry", None), P(("val", "qry"), None), P(("val", "qry"), None)),
        check_vma=False,
    )
```

```python
import jax
import jax.numpy as jnp
from jax import lax
from jax.experimental import pallas as pl
from jax.experimental.pallas import tpu as pltpu
from jax.sharding import PartitionSpec as P

ZH, Y, CORES, ZL, X = 4, 8, 2, 2, 4
UP, DOWN = 4, 3
CHUNKS, POOL_WAIT = 2, 4
MESH = pl.DeviceIdType.MESH
VMEM = pl.BlockSpec(memory_space=pltpu.VMEM)


def place():
    val, qry = lax.axis_index("val"), lax.axis_index("qry")
    core, y, zh = val % CORES, (val // CORES) % Y, val // (CORES * Y)
    return core, y, zh, qry // X, qry % X


def device(core, y, zh, zl, x):
    return ((zh * Y + y) * CORES + core, zl * X + x)


def neighbours():
    core, y, zh, zl, x = place()
    across = device(1 - core, y, zh, zl, x)
    along_y = [device(core, (y + d) % Y, zh, zl, x) for d in range(1, Y)]
    along_z = [device(core, y, (zh + d) % ZH, zl, x) for d in range(1, ZH)]
    along_x = [device(core, y, zh, zl, (x + d) % X) for d in range(1, X)]
    beside = device(core, y, zh, 1 - zl, x)
    return across, along_y, along_z, along_x, beside


def mult(first, size):
    return pl.ds(pl.multiple_of(first, size), size)


def dot(a, b, dims):
    return lax.dot_general(a, b, ((dims[:1], dims[1:]), ((), ())), preferred_element_type=jnp.float32)


def push(src, dst, send, recv, there):
    copy = pltpu.make_async_remote_copy(
        src_ref=src, dst_ref=dst, send_sem=send, recv_sem=recv, device_id=there, device_id_type=MESH
    )
    copy.start()
    return copy


def backward_kernel(
    queries, grads, keys, values, lse, targets, compat, query_out, key_out, value_out,
    probs, weights, delta, delta_core, delta_sum, delta_y, delta_line, delta_z, query, sums, key_sums, pool,
    from_core, up_in, down_in, up_out, down_out, sum_y, from_z, mine, line,
    from_x, sum_x, from_beside, send, recv,
):
    f32, low = jnp.float32, jnp.bfloat16
    core, y, zh, zl, x = place()
    across, along_y, along_z, along_x, beside = neighbours()
    upper, lower = along_y[0], along_y[-1]
    friends = [across] + along_y + along_z + along_x + [beside]
    barrier = pltpu.get_barrier_semaphore()
    for there in friends:
        pl.semaphore_signal(barrier, inc=1, device_id=there, device_id_type=MESH)

    count, columns = queries.shape
    tiles, tile = delta.shape
    value_count = keys.shape[0]
    offset = lax.axis_index("val") * value_count
    heads = probs.shape[0]
    head_width = columns // heads
    per_head = tiles // heads
    scale = head_width ** (-0.5)
    half = from_core.shape[1]
    piece = half // Y
    width = columns // ZH
    share = key_out.shape[0]
    own_columns = mult(zh * width, width)
    done = []
    used = iter(range(send.shape[0]))

    def start(src, dst, there):
        n = next(used)
        copy = push(src, dst, send.at[n], recv.at[n], there)
        done.append(copy)
        return copy

    def head_columns(h):
        return pl.ds(h * head_width, head_width)

    for h in range(heads):
        cols = head_columns(h)
        sums[...] = jnp.zeros_like(sums)

        def first_pass(b, carry):
            rows = mult(b * tile, tile)
            grad_tile = grads[rows, cols]
            local = targets[pl.ds(h, 1), rows] - offset
            mark = jnp.full(local.shape, compat[h, b], jnp.int32)
            usable = (mark == 1) | ((local >= 0) & (local < value_count))
            lse_row = jnp.where(usable, lse[pl.ds(h, 1), rows], 3e38)
            scores = dot(keys[:, cols], queries[rows, cols], (1, 1)) * scale
            p = jnp.exp(scores - lse_row)
            dprobs = dot(values[:, cols], grad_tile, (1, 1))
            terms = p * dprobs
            delta[pl.ds(h * per_head + b, 1), :] = jnp.sum(terms, axis=0, keepdims=True)
            slot = lax.broadcasted_iota(jnp.int32, p.shape, 0)
            hit = slot == local
            probs[h, :, rows] = p
            weights[h, :, rows] = terms + p - jnp.where(hit, 1.0, 0.0)
            sums[...] += dot(p.astype(low), grad_tile, (1, 0))
            return carry

        lax.fori_loop(0, per_head, first_pass, 0, unroll=3)
        for r in range(ZL * X):
            pool[1, r // X, r % X, :, cols] = sums[pl.ds(r * share, share), :].astype(low)

    pl.semaphore_wait(barrier, len(friends))

    def pool_steps(n, out, wait):
        x_stage = [
            start(pool.at[n, :, (x + d) % X], from_x.at[n, d - 1], there)
            for d, there in zip(range(1, X), along_x)
        ]
        for _ in range(wait):
            yield
        acc = pool[n, :, x].astype(f32)
        for d, copy in enumerate(x_stage):
            copy.wait_recv()
            acc = acc + from_x[n, d].astype(f32)
        sum_x[n] = acc.astype(low)
        copy = start(sum_x.at[n, 1 - zl], from_beside.at[n], beside)
        for _ in range(3):
            yield
        copy.wait_recv()
        out[...] = (sum_x[n, zl].astype(f32) + from_beside[n].astype(f32)).astype(low)

    swap = start(delta, delta_core, across)
    swap.wait_recv()
    delta_sum[...] = delta[...] + delta_core[...]
    stage = [start(delta_sum, delta_y.at[d], there) for d, there in enumerate(along_y)]
    value_lane = pool_steps(1, value_out, 1)
    next(value_lane)
    acc = delta_sum[...]
    for d, copy in enumerate(stage):
        copy.wait_recv()
        acc = acc + delta_y[d]
    delta_line[...] = acc
    stage = [start(delta_line, delta_z.at[d], there) for d, there in enumerate(along_z)]
    for d, copy in enumerate(stage):
        copy.wait_recv()
        acc = acc + delta_z[d]
    delta_core[...] = acc

    def rows(k, c, owner):
        first = k * CORES * half + c * half + lax.rem(owner + Y, Y) * piece
        return pl.ds(pl.multiple_of(first, piece), piece)

    def half_rows(k, c):
        return pl.ds(pl.multiple_of(k * CORES * half + c * half, half), half)

    def own(k, owner):
        inside = pl.ds(pl.multiple_of(lax.rem(owner + Y, Y) * piece, piece), piece)
        return query[rows(k, core, owner), :].astype(f32) + from_core[k, inside, :].astype(f32)

    def query_steps(k):
        swap = start(query.at[half_rows(k, 1 - core)], from_core.at[k], across)
        yield
        swap.wait_recv()
        up_out[k, 0] = own(k, y + UP).astype(low)
        up = start(up_out.at[k, 0], up_in.at[k, 0], upper)
        down_out[k, 0] = own(k, y - DOWN).astype(low)
        down = start(down_out.at[k, 0], down_in.at[k, 0], lower)
        for s in range(1, UP):
            yield
            up.wait_recv()
            up_out[k, s] = (own(k, y + UP - s) + up_in[k, s - 1].astype(f32)).astype(low)
            up = start(up_out.at[k, s], up_in.at[k, s], upper)
            if s < DOWN:
                down.wait_recv()
                down_out[k, s] = (own(k, y - DOWN + s) + down_in[k, s - 1].astype(f32)).astype(low)
                down = start(down_out.at[k, s], down_in.at[k, s], lower)
        yield
        down.wait_recv()
        up.wait_recv()
        total = own(k, y) + up_in[k, UP - 1].astype(f32) + down_in[k, DOWN - 1].astype(f32)
        sum_y[k] = total.astype(low)
        z_stage = [
            start(
                sum_y.at[k, :, pl.ds(pl.multiple_of((zh + d) % ZH * width, width), width)],
                from_z.at[k, d - 1],
                there,
            )
            for d, there in zip(range(1, ZH), along_z)
        ]
        yield
        acc = sum_y[k, :, own_columns].astype(f32)
        for d, copy in enumerate(z_stage):
            copy.wait_recv()
            acc = acc + from_z[k, d].astype(f32)
        mine[k] = acc.astype(low)
        back_z = [start(mine.at[k], line.at[k, :, own_columns], there) for there in along_z]
        line[k, :, own_columns] = mine[k]
        yield
        for copy in back_z:
            copy.wait_recv()
        here = rows(k, core, y)
        up = start(line.at[k], query_out.at[here], upper)
        down = start(line.at[k], query_out.at[here], lower)
        query_out[here, :] = line[k]
        back_core = [start(line.at[k], query_out.at[here], across)]
        for s in range(1, UP + 1):
            yield
            up.wait_recv()
            got = query_out.at[rows(k, core, y - s)]
            if s < UP:
                up = start(got, got, upper)
            forward = [got]
            if s <= DOWN:
                down.wait_recv()
                got = query_out.at[rows(k, core, y + s)]
                if s < DOWN:
                    down = start(got, got, lower)
                forward.append(got)
            back_core += [start(got, got, across) for got in forward]
        yield
        for copy in back_core:
            copy.wait_recv()

    def second_pass(k, h):
        cols = head_columns(h)

        def step(b, carry):
            rows = mult(b * tile, tile)
            d = delta_core[pl.ds(h * per_head + b, 1), :]
            dscores = (weights[h, :, rows] - probs[h, :, rows] * d).astype(low)
            query[rows, cols] = (dot(dscores, keys[:, cols], (0, 0)) * scale).astype(low)
            key_sums[:, cols] += dot(dscores, queries[rows, cols], (1, 0))
            return carry

        per_chunk = per_head // CHUNKS
        lax.fori_loop(k * per_chunk, (k + 1) * per_chunk, step, 0, unroll=3)

    key_sums[...] = jnp.zeros_like(key_sums)
    lanes = [value_lane]
    for k in range(CHUNKS):
        for h in range(heads):
            second_pass(k, h)
        lanes.append(query_steps(k))
        next(lanes[-1])
    for r in range(ZL * X):
        pool[0, r // X, r % X] = (key_sums[pl.ds(r * share, share), :] * scale).astype(low)
    lanes.append(pool_steps(0, key_out, POOL_WAIT))
    while lanes:
        lanes = [steps for steps in lanes if next(steps, lanes) is not lanes]
    for copy in done:
        copy.wait_send()


def on_device(queries, pool_keys, pool_values, out_grad, lse, compat, targets):
    heads, _, query_blocks = compat.shape
    count, columns = queries.shape
    value_count = pool_keys.shape[0]
    query_block = count // query_blocks
    tiles = heads * query_blocks
    low, f32 = jnp.bfloat16, jnp.float32
    share = value_count // (ZL * X)
    half = count // (CORES * CHUNKS)
    piece = half // Y
    width = columns // ZH
    copies = CHUNKS * (1 + (Y - 1) + (ZH - 1) * 2 + (Y - 1) + Y) + 2 * X + 1 + (Y - 1) + (ZH - 1)
    row = (tiles, query_block)
    return pl.pallas_call(
        backward_kernel,
        out_shape=(
            jax.ShapeDtypeStruct(queries.shape, low),
            jax.ShapeDtypeStruct((share, columns), low),
            jax.ShapeDtypeStruct((share, columns), low),
        ),
        in_specs=[VMEM] * 6 + [pl.BlockSpec(memory_space=pltpu.SMEM)],
        out_specs=(VMEM, VMEM, VMEM),
        scratch_shapes=[
            pltpu.VMEM((heads, value_count, count), f32),
            pltpu.VMEM((heads, value_count, count), f32),
            pltpu.VMEM(row, f32),
            pltpu.VMEM(row, f32),
            pltpu.VMEM(row, f32),
            pltpu.VMEM((Y - 1, *row), f32),
            pltpu.VMEM(row, f32),
            pltpu.VMEM((ZH - 1, *row), f32),
            pltpu.VMEM(queries.shape, low),
            pltpu.VMEM((value_count, columns // heads), f32),
            pltpu.VMEM((value_count, columns), f32),
            pltpu.VMEM((2, ZL, X, share, columns), low),
            pltpu.VMEM((CHUNKS, half, columns), low),
            pltpu.VMEM((CHUNKS, UP, piece, columns), low),
            pltpu.VMEM((CHUNKS, DOWN, piece, columns), low),
            pltpu.VMEM((CHUNKS, UP, piece, columns), low),
            pltpu.VMEM((CHUNKS, DOWN, piece, columns), low),
            pltpu.VMEM((CHUNKS, piece, columns), low),
            pltpu.VMEM((CHUNKS, ZH - 1, piece, width), low),
            pltpu.VMEM((CHUNKS, piece, width), low),
            pltpu.VMEM((CHUNKS, piece, columns), low),
            pltpu.VMEM((2, X - 1, ZL, share, columns), low),
            pltpu.VMEM((2, ZL, share, columns), low),
            pltpu.VMEM((2, share, columns), low),
            pltpu.SemaphoreType.DMA((copies,)),
            pltpu.SemaphoreType.DMA((copies,)),
        ],
        compiler_params=pltpu.CompilerParams(
            collective_id=0, has_side_effects=True, vmem_limit_bytes=56 * 1024 * 1024
        ),
    )(queries, out_grad, pool_keys, pool_values, lse, jnp.transpose(targets), compat[:, 0, :])


def solution(mesh):
    placed = (
        P("qry", None),
        P("val", None),
        P("val", None),
        P("qry", None),
        P(None, "qry"),
        P(None, "val", "qry"),
        P("qry", None),
    )
    return jax.shard_map(
        on_device,
        mesh=mesh,
        in_specs=placed,
        out_specs=(P("qry", None), P(("val", "qry"), None), P(("val", "qry"), None)),
        check_vma=False,
    )
```

```python
import jax
import jax.numpy as jnp
from jax import lax
from jax.experimental import pallas as pl
from jax.experimental.pallas import tpu as pltpu
from jax.sharding import PartitionSpec as P

ZH, Y, CORES, ZL, X = 4, 8, 2, 2, 4
UP, DOWN = 4, 3
CHUNKS, POOL_WAIT = 2, 4
MESH = pl.DeviceIdType.MESH
VMEM = pl.BlockSpec(memory_space=pltpu.VMEM)


def place():
    val, qry = lax.axis_index("val"), lax.axis_index("qry")
    core, y, zh = val % CORES, (val // CORES) % Y, val // (CORES * Y)
    return core, y, zh, qry // X, qry % X


def device(core, y, zh, zl, x):
    return ((zh * Y + y) * CORES + core, zl * X + x)


def neighbours():
    core, y, zh, zl, x = place()
    across = device(1 - core, y, zh, zl, x)
    along_y = [device(core, (y + d) % Y, zh, zl, x) for d in range(1, Y)]
    along_z = [device(core, y, (zh + d) % ZH, zl, x) for d in range(1, ZH)]
    along_x = [device(core, y, zh, zl, (x + d) % X) for d in range(1, X)]
    beside = device(core, y, zh, 1 - zl, x)
    return across, along_y, along_z, along_x, beside


def mult(first, size):
    return pl.ds(pl.multiple_of(first, size), size)


def dot(a, b, dims):
    return lax.dot_general(a, b, ((dims[:1], dims[1:]), ((), ())), preferred_element_type=jnp.float32)


def push(src, dst, send, recv, there):
    copy = pltpu.make_async_remote_copy(
        src_ref=src, dst_ref=dst, send_sem=send, recv_sem=recv, device_id=there, device_id_type=MESH
    )
    copy.start()
    return copy


def backward_kernel(
    queries, grads, keys, values, lse, targets, compat, query_out, key_out, value_out,
    probs, weights, delta, delta_core, delta_sum, delta_y, delta_line, delta_z, query, sums, key_sums, pool,
    from_core, up_in, down_in, up_out, down_out, sum_y, from_z, mine, line,
    from_x, sum_x, from_beside, send, recv,
):
    f32, low = jnp.float32, jnp.bfloat16
    core, y, zh, zl, x = place()
    across, along_y, along_z, along_x, beside = neighbours()
    upper, lower = along_y[0], along_y[-1]
    friends = [across] + along_y + along_z + along_x + [beside]
    barrier = pltpu.get_barrier_semaphore()
    for there in friends:
        pl.semaphore_signal(barrier, inc=1, device_id=there, device_id_type=MESH)

    count, columns = queries.shape
    tiles, tile = delta.shape
    value_count = keys.shape[0]
    offset = lax.axis_index("val") * value_count
    heads = probs.shape[0]
    head_width = columns // heads
    per_head = tiles // heads
    scale = head_width ** (-0.5)
    half = from_core.shape[1]
    piece = half // Y
    width = columns // ZH
    share = key_out.shape[0]
    own_columns = mult(zh * width, width)
    done = []
    used = iter(range(send.shape[0]))

    def start(src, dst, there):
        n = next(used)
        copy = push(src, dst, send.at[n], recv.at[n], there)
        done.append(copy)
        return copy

    def head_columns(h):
        return pl.ds(h * head_width, head_width)

    for h in range(heads):
        cols = head_columns(h)
        sums[...] = jnp.zeros_like(sums)

        def first_pass(b, carry):
            rows = mult(b * tile, tile)
            grad_tile = grads[rows, cols]
            local = targets[pl.ds(h, 1), rows] - offset
            mark = jnp.full(local.shape, compat[h, b], jnp.int32)
            usable = (mark == 1) | ((local >= 0) & (local < value_count))
            lse_row = jnp.where(usable, lse[pl.ds(h, 1), rows], 3e38)
            scores = dot(keys[:, cols], queries[rows, cols], (1, 1)) * scale
            p = jnp.exp(scores - lse_row)
            dprobs = dot(values[:, cols], grad_tile, (1, 1))
            terms = p * dprobs
            delta[pl.ds(h * per_head + b, 1), :] = jnp.sum(terms, axis=0, keepdims=True)
            slot = lax.broadcasted_iota(jnp.int32, p.shape, 0)
            hit = slot == local
            probs[h, :, rows] = p
            weights[h, :, rows] = terms + p - jnp.where(hit, 1.0, 0.0)
            sums[...] += dot(p.astype(low), grad_tile, (1, 0))
            return carry

        lax.fori_loop(0, per_head, first_pass, 0, unroll=True)
        for r in range(ZL * X):
            pool[1, r // X, r % X, :, cols] = sums[pl.ds(r * share, share), :].astype(low)

    pl.semaphore_wait(barrier, len(friends))

    def pool_steps(n, out, wait):
        x_stage = [
            start(pool.at[n, :, (x + d) % X], from_x.at[n, d - 1], there)
            for d, there in zip(range(1, X), along_x)
        ]
        for _ in range(wait):
            yield
        acc = pool[n, :, x].astype(f32)
        for d, copy in enumerate(x_stage):
            copy.wait_recv()
            acc = acc + from_x[n, d].astype(f32)
        sum_x[n] = acc.astype(low)
        copy = start(sum_x.at[n, 1 - zl], from_beside.at[n], beside)
        for _ in range(3):
            yield
        copy.wait_recv()
        out[...] = (sum_x[n, zl].astype(f32) + from_beside[n].astype(f32)).astype(low)

    swap = start(delta, delta_core, across)
    swap.wait_recv()
    delta_sum[...] = delta[...] + delta_core[...]
    stage = [start(delta_sum, delta_y.at[d], there) for d, there in enumerate(along_y)]
    value_lane = pool_steps(1, value_out, 1)
    next(value_lane)
    acc = delta_sum[...]
    for d, copy in enumerate(stage):
        copy.wait_recv()
        acc = acc + delta_y[d]
    delta_line[...] = acc
    stage = [start(delta_line, delta_z.at[d], there) for d, there in enumerate(along_z)]
    for d, copy in enumerate(stage):
        copy.wait_recv()
        acc = acc + delta_z[d]
    delta_core[...] = acc

    def rows(k, c, owner):
        first = k * CORES * half + c * half + lax.rem(owner + Y, Y) * piece
        return pl.ds(pl.multiple_of(first, piece), piece)

    def half_rows(k, c):
        return pl.ds(pl.multiple_of(k * CORES * half + c * half, half), half)

    def own(k, owner):
        inside = pl.ds(pl.multiple_of(lax.rem(owner + Y, Y) * piece, piece), piece)
        return query[rows(k, core, owner), :].astype(f32) + from_core[k, inside, :].astype(f32)

    def query_steps(k):
        swap = start(query.at[half_rows(k, 1 - core)], from_core.at[k], across)
        yield
        swap.wait_recv()
        up_out[k, 0] = own(k, y + UP).astype(low)
        up = start(up_out.at[k, 0], up_in.at[k, 0], upper)
        down_out[k, 0] = own(k, y - DOWN).astype(low)
        down = start(down_out.at[k, 0], down_in.at[k, 0], lower)
        for s in range(1, UP):
            yield
            up.wait_recv()
            up_out[k, s] = (own(k, y + UP - s) + up_in[k, s - 1].astype(f32)).astype(low)
            up = start(up_out.at[k, s], up_in.at[k, s], upper)
            if s < DOWN:
                down.wait_recv()
                down_out[k, s] = (own(k, y - DOWN + s) + down_in[k, s - 1].astype(f32)).astype(low)
                down = start(down_out.at[k, s], down_in.at[k, s], lower)
        yield
        down.wait_recv()
        up.wait_recv()
        total = own(k, y) + up_in[k, UP - 1].astype(f32) + down_in[k, DOWN - 1].astype(f32)
        sum_y[k] = total.astype(low)
        z_stage = [
            start(
                sum_y.at[k, :, pl.ds(pl.multiple_of((zh + d) % ZH * width, width), width)],
                from_z.at[k, d - 1],
                there,
            )
            for d, there in zip(range(1, ZH), along_z)
        ]
        yield
        acc = sum_y[k, :, own_columns].astype(f32)
        for d, copy in enumerate(z_stage):
            copy.wait_recv()
            acc = acc + from_z[k, d].astype(f32)
        mine[k] = acc.astype(low)
        back_z = [start(mine.at[k], line.at[k, :, own_columns], there) for there in along_z]
        line[k, :, own_columns] = mine[k]
        yield
        for copy in back_z:
            copy.wait_recv()
        here = rows(k, core, y)
        up = start(line.at[k], query_out.at[here], upper)
        down = start(line.at[k], query_out.at[here], lower)
        query_out[here, :] = line[k]
        back_core = [start(line.at[k], query_out.at[here], across)]
        for s in range(1, UP + 1):
            yield
            up.wait_recv()
            got = query_out.at[rows(k, core, y - s)]
            if s < UP:
                up = start(got, got, upper)
            forward = [got]
            if s <= DOWN:
                down.wait_recv()
                got = query_out.at[rows(k, core, y + s)]
                if s < DOWN:
                    down = start(got, got, lower)
                forward.append(got)
            back_core += [start(got, got, across) for got in forward]
        yield
        for copy in back_core:
            copy.wait_recv()

    def second_pass(k, h):
        cols = head_columns(h)

        def step(b, carry):
            rows = mult(b * tile, tile)
            d = delta_core[pl.ds(h * per_head + b, 1), :]
            dscores = (weights[h, :, rows] - probs[h, :, rows] * d).astype(low)
            query[rows, cols] = (dot(dscores, keys[:, cols], (0, 0)) * scale).astype(low)
            key_sums[:, cols] += dot(dscores, queries[rows, cols], (1, 0))
            return carry

        per_chunk = per_head // CHUNKS
        lax.fori_loop(k * per_chunk, (k + 1) * per_chunk, step, 0, unroll=3)

    key_sums[...] = jnp.zeros_like(key_sums)
    lanes = [value_lane]
    for k in range(CHUNKS):
        for h in range(heads):
            second_pass(k, h)
            if k > 0 and h == 0:
                next(lanes[k])
        lanes.append(query_steps(k))
        next(lanes[-1])
    for r in range(ZL * X):
        pool[0, r // X, r % X] = (key_sums[pl.ds(r * share, share), :] * scale).astype(low)
    lanes.append(pool_steps(0, key_out, POOL_WAIT))
    while lanes:
        lanes = [steps for steps in lanes if next(steps, lanes) is not lanes]
    for copy in done:
        copy.wait_send()


def on_device(queries, pool_keys, pool_values, out_grad, lse, compat, targets):
    heads, _, query_blocks = compat.shape
    count, columns = queries.shape
    value_count = pool_keys.shape[0]
    query_block = count // query_blocks
    tiles = heads * query_blocks
    low, f32 = jnp.bfloat16, jnp.float32
    share = value_count // (ZL * X)
    half = count // (CORES * CHUNKS)
    piece = half // Y
    width = columns // ZH
    copies = CHUNKS * (1 + (Y - 1) + (ZH - 1) * 2 + (Y - 1) + Y) + 2 * X + 1 + (Y - 1) + (ZH - 1)
    row = (tiles, query_block)
    return pl.pallas_call(
        backward_kernel,
        out_shape=(
            jax.ShapeDtypeStruct(queries.shape, low),
            jax.ShapeDtypeStruct((share, columns), low),
            jax.ShapeDtypeStruct((share, columns), low),
        ),
        in_specs=[VMEM] * 6 + [pl.BlockSpec(memory_space=pltpu.SMEM)],
        out_specs=(VMEM, VMEM, VMEM),
        scratch_shapes=[
            pltpu.VMEM((heads, value_count, count), f32),
            pltpu.VMEM((heads, value_count, count), f32),
            pltpu.VMEM(row, f32),
            pltpu.VMEM(row, f32),
            pltpu.VMEM(row, f32),
            pltpu.VMEM((Y - 1, *row), f32),
            pltpu.VMEM(row, f32),
            pltpu.VMEM((ZH - 1, *row), f32),
            pltpu.VMEM(queries.shape, low),
            pltpu.VMEM((value_count, columns // heads), f32),
            pltpu.VMEM((value_count, columns), f32),
            pltpu.VMEM((2, ZL, X, share, columns), low),
            pltpu.VMEM((CHUNKS, half, columns), low),
            pltpu.VMEM((CHUNKS, UP, piece, columns), low),
            pltpu.VMEM((CHUNKS, DOWN, piece, columns), low),
            pltpu.VMEM((CHUNKS, UP, piece, columns), low),
            pltpu.VMEM((CHUNKS, DOWN, piece, columns), low),
            pltpu.VMEM((CHUNKS, piece, columns), low),
            pltpu.VMEM((CHUNKS, ZH - 1, piece, width), low),
            pltpu.VMEM((CHUNKS, piece, width), low),
            pltpu.VMEM((CHUNKS, piece, columns), low),
            pltpu.VMEM((2, X - 1, ZL, share, columns), low),
            pltpu.VMEM((2, ZL, share, columns), low),
            pltpu.VMEM((2, share, columns), low),
            pltpu.SemaphoreType.DMA((copies,)),
            pltpu.SemaphoreType.DMA((copies,)),
        ],
        compiler_params=pltpu.CompilerParams(
            collective_id=0, has_side_effects=True, vmem_limit_bytes=56 * 1024 * 1024
        ),
    )(queries, out_grad, pool_keys, pool_values, lse, jnp.transpose(targets), compat[:, 0, :])


def solution(mesh):
    placed = (
        P("qry", None),
        P("val", None),
        P("val", None),
        P("qry", None),
        P(None, "qry"),
        P(None, "val", "qry"),
        P("qry", None),
    )
    return jax.shard_map(
        on_device,
        mesh=mesh,
        in_specs=placed,
        out_specs=(P("qry", None), P(("val", "qry"), None), P(("val", "qry"), None)),
        check_vma=False,
    )
```
